32 devices in a mesh: groups: 2 (over x), row: 8 (over z, y), col: 2 (over core).
Axes of the slice: x: 2, y: 2, z: 4, core: 2. Of those that a mesh axis runs over, the one named last changes fastest.
Arguments:
- inverse: float32 [16, 2, 128, 2048], P('groups', 'col', None, 'row'), parts along dimension 0, as said below
- features: float32 [16384, 1024], P(('groups', 'row')), parts along dimension 0, may hold values from -6 to 6
- residual: float32 [16384, 256], P(('groups', 'row')), parts along dimension 0, may hold values from -6 to 6
- block_ids: int32 [4096], P(('groups', 'row')), parts along dimension 0, may hold values from 0 to 8191, as said below
Outputs:
- updated: float32 [16384, 256], P(('groups', 'row'), 'col'), parts along dimension 0
The draws below stay inside these ranges and needn't reach their ends.
There are 2 independent parts, one for each index of `groups`. The reference program is written for one: setup_inputs(seed, part) draws one part's arguments, and reference() takes and returns one part's arrays. A program takes and returns all parts, laid end to end along the dimension named above; each array names one. Nothing has to cross between parts.
Inputs may be any that keep to these rules, and one draw needn't show every extreme that they name: `block_ids`: the ids at block positions a * 256 to (a + 1) * 256 - 1 are distinct and lie in a * 1024 to (a + 1) * 1024 - 1. `inverse`: read as a [2048, 2048] matrix, each row is a positive scale between 0.3 and 3.4 times an identity row plus small independent entries.
All inputs are finite; a program needn't handle non-finite values.
Results may differ from the reference program's by a relative error of at most 0.000084.
Values sent between devices are 32-bit elements; how exact they have to be, the bound alone decides.
No kernel may reach another device: no remote copies, remote signals or barrier semaphores. Data moves between devices by JAX's collectives and lax.ppermute only.
A program may use at most 128 MiB of HBM per device.

```python
import jax
import jax.numpy as jnp
from jax import lax

F = 1024
R = 256
BLK_DEV = 256
ROWS_DEV = 1024
HALF = 128
B = 2048
M = 8192


def draw_inverse(key, part):
    scale = 0.6 / B ** 0.5
    entries = jax.random.normal(jax.random.fold_in(key, 13), (B, B), jnp.float32)
    full = entries * scale + jnp.eye(B, dtype=jnp.float32)
    return full.reshape(B // BLK_DEV, BLK_DEV // HALF, HALF, B)


def draw_block_ids(key, part):
    groups_count = B // BLK_DEV
    keys = jax.random.split(jax.random.fold_in(key, 21), groups_count)
    picked = jax.vmap(lambda k: jax.random.permutation(k, ROWS_DEV)[:BLK_DEV])(keys)
    offsets = (jnp.arange(groups_count, dtype=jnp.int32) * ROWS_DEV)[:, None]
    return (picked.astype(jnp.int32) + offsets).reshape(B)


def shard_levels(rng, dims, cuts, least, high):
    level, own = 1.0, jax.random.fold_in(rng, 6)
    for position, parts in cuts:
        draws = jnp.exp(jax.random.uniform(jax.random.fold_in(own, position), (parts,), jnp.float32, least / len(cuts), high / len(cuts)))
        level = level * jnp.repeat(draws, dims[position] // parts).reshape([-1 if axis == position else 1 for axis in range(len(dims))])
    return level


def gaussian(own_key, dims, deviation, most, cuts=(), kind=jnp.bfloat16):
    result = deviation * jax.random.normal(own_key, dims, jnp.float32)
    if cuts:
        result = result * shard_levels(own_key, dims, cuts, -0.22, 0.18)
    return jnp.clip(result, -most, most).astype(kind)


def setup_inputs(seed: int = 0, part: int = 0) -> dict:
    seeds = jax.random.split(jax.random.key(seed), 5)
    part_splits = jax.random.split(jax.random.fold_in(seeds[4], part), 5)
    inverse = draw_inverse(jax.random.fold_in(jax.random.fold_in(seeds[4], part), 71), part)
    features = gaussian(part_splits[1], (M, F), 1.0, 6.0, ((0, 8),), jnp.float32)
    residual = gaussian(part_splits[2], (M, R), 1.0, 6.0, ((0, 8),), jnp.float32)
    block_ids = draw_block_ids(jax.random.fold_in(jax.random.fold_in(seeds[4], part), 71), part)
    return {"inverse": inverse, "features": features, "residual": residual, "block_ids": block_ids}


def kernel_rows(rows_x, block_x, correction):
    gram = jnp.dot(rows_x, block_x.T, precision=lax.Precision.HIGHEST, preferred_element_type=jnp.float32)
    kern = (gram / F + 0.5) ** 2
    return jnp.dot(kern, correction, precision=lax.Precision.HIGHEST, preferred_element_type=jnp.float32)


def reference(inverse, features, residual, block_ids):
    inv = inverse.reshape(B, B)
    block_res = jnp.take(residual, block_ids, axis=0)
    correction = jnp.dot(inv, block_res, precision=lax.Precision.HIGHEST, preferred_element_type=jnp.float32)
    block_x = jnp.take(features, block_ids, axis=0)
    blocks = features.reshape(M // ROWS_DEV, ROWS_DEV, F)
    change = lax.map(lambda rows_x: kernel_rows(rows_x, block_x, correction), blocks)
    return residual - change.reshape(M, R)
```

```python
import numpy as np
import jax
import jax.numpy as jnp
from jax import lax
from jax.sharding import PartitionSpec as P

HIGH = lax.Precision.HIGH


def dot(a, b, dims=(((1,), (0,)), ((), ()))):
    return lax.dot_general(a, b, dims, precision=HIGH, preferred_element_type=jnp.float32)


def line_streams(own, depth, width):
    def shift(x, sources, step):
        pairs = [((z * width + y), ((z + step) * width + y)) for z in sources for y in range(width)]
        return lax.ppermute(x, "row", pairs)

    def across(x, places):
        pairs = [(z * width + y, z * width + (width - 1 - y)) for z in places for y in range(width)]
        return lax.ppermute(x, "row", pairs)

    got, crossed = {}, {}
    up = down = own
    crossed[0] = across(own, range(depth)) if width > 1 else None
    for s in range(1, depth):
        up = got[-s] = shift(up, range(s - 1, depth - 1), 1)
        down = got[s] = shift(down, range(1, depth - s + 1), -1)
        if width > 1:
            crossed[-s] = across(up, range(s, depth))
            crossed[s] = across(down, range(0, depth - s))
    return got, crossed


def arrivals(depth):
    table = []
    for z in range(depth):
        order = [(s, -s) for s in range(1, depth) if z - s >= 0] + [(s, s) for s in range(1, depth) if z + s < depth]
        table.append([off for _, off in sorted(order, key=lambda e: (e[0], e[1] > 0))])
    return np.array(table, np.int32).reshape(depth, depth - 1)


def pick(z, column, parts):
    out = None
    for off in sorted(set(column.tolist())):
        here = parts[off]
        if out is None:
            out = here
        else:
            mask = jnp.asarray((column == off))[z]
            out = jnp.where(mask, here, out)
    return out


def reduce_all(blocks, bits):
    n = len(blocks)
    pairs_of = {b: [(r, r ^ b) for r in range(n)] for b in bits}
    live = {k: blocks[k] for k in range(n)}
    for b in bits:
        send = [k for k in sorted(live) if k & b]
        moved = lax.ppermute(jnp.concatenate([live[k] for k in send], 0), "row", pairs_of[b])
        rows = live[send[0]].shape[0]
        live = {k ^ b: live[k ^ b] + moved[i * rows:(i + 1) * rows] for i, k in enumerate(send)}
    for b in reversed(bits):
        have = sorted(live)
        moved = lax.ppermute(jnp.concatenate([live[k] for k in have], 0), "row", pairs_of[b])
        rows = live[have[0]].shape[0]
        for i, k in enumerate(have):
            live[k ^ b] = moved[i * rows:(i + 1) * rows]
    return jnp.stack([live[k] for k in range(n)])


def on_device(inverse, features, residual, block_ids):
    n = lax.axis_size("row")
    me, col = lax.axis_index("row"), lax.axis_index("col")
    cols = lax.axis_size("col")
    width = 2 if n % 2 == 0 else 1
    depth = n // width
    z, y = me // width, me % width
    rows_here, feats = features.shape
    local_ids = block_ids - me * rows_here
    half = block_ids.shape[0] // cols
    own_ids = lax.dynamic_slice_in_dim(local_ids, col * half, half)
    own_x = jnp.take(features, own_ids, axis=0, mode="clip")
    block_res = jnp.take(residual, local_ids, axis=0, mode="clip")

    partial = dot(inverse.reshape(-1, inverse.shape[-1]), block_res).reshape(n, half, -1)
    relative = jnp.take(partial, me ^ jnp.arange(n), axis=0, mode="clip")
    rhs = partial.shape[-1] // cols
    bits = [1 << i for i in range(n.bit_length() - 1)]
    orders = [bits[1:] + bits[:1], bits]
    sums = []
    for h in range(cols):
        part = relative[:, :, h * rhs:(h + 1) * rhs]
        sums.append(reduce_all([part[k] for k in range(n)], orders[h % 2]))

    got, crossed = line_streams(own_x, depth, width)
    table = arrivals(depth)
    got[0] = own_x

    def kern(xs):
        gram = dot(features, jnp.concatenate(xs, 0), (((1,), (1,)), ((), ())))
        return (gram / feats + 0.5) ** 2

    kerns, owners = [], []
    for j in range(-1, depth - 1):
        column = np.zeros(depth, np.int32) if j < 0 else table[:, j]
        xs = [pick(z, column, got)]
        place = z + jnp.asarray(column)[z]
        owners.append(place * width + y)
        if width > 1:
            xs.append(pick(z, column, crossed))
            owners.append(place * width + (width - 1 - y))
        kerns.append(kern(xs))
    kernel = jnp.concatenate(kerns, 1)
    order = jnp.stack(owners) ^ me
    corr = [jnp.take(s, order, axis=0, mode="clip").reshape(-1, rhs) for s in sums]
    other = jnp.where(col == 0, corr[1], corr[0])
    mine = jnp.where(col == 0, corr[0], corr[1])
    theirs = lax.ppermute(dot(kernel, other), "col", [(c, cols - 1 - c) for c in range(cols)])
    own_res = lax.dynamic_slice_in_dim(residual, col * rhs, rhs, 1)
    return own_res - (dot(kernel, mine) + theirs)


def solution(mesh):
    return jax.shard_map(
        on_device,
        mesh=mesh,
        in_specs=(
            P("groups", "col", None, "row"),
            P(("groups", "row"), None),
            P(("groups", "row"), None),
            P(("groups", "row")),
        ),
        out_specs=P(("groups", "row"), "col"),
        check_vma=False,
    )
```

```python
import jax
import jax.numpy as jnp
from jax import lax
from jax.experimental import pallas as pl
from jax.experimental.pallas import tpu as pltpu
from jax.sharding import PartitionSpec as P

F32, BF16 = jnp.float32, jnp.bfloat16
NT = (((1,), (1,)), ((), ()))
NN = (((1,), (0,)), ((), ()))
WIDTH = 2


def mm(a, b, dims):
    return lax.dot_general(a, b, dims, preferred_element_type=F32)


def halves(x):
    high = x.astype(BF16)
    return high, (x - high.astype(F32)).astype(BF16)


VMEM = pl.BlockSpec(memory_space=pltpu.VMEM)
PARAMS = pltpu.CompilerParams(vmem_limit_bytes=8 << 20)


def in_vmem(*arrays):
    return [pltpu.with_memory_space_constraint(a, pltpu.VMEM) for a in arrays]


def split_kernel(x_ref, high_ref, low_ref):
    high_ref[...], low_ref[...] = halves(x_ref[...])


def split(x, tile=256):
    rows, cols = x.shape
    return pl.pallas_call(
        split_kernel,
        grid=(rows // tile,),
        in_specs=[pl.BlockSpec((tile, cols), lambda i: (i, 0))],
        out_specs=[pl.BlockSpec((tile, cols), lambda i: (i, 0))] * 2,
        out_shape=[pltpu.VMEM(x.shape, BF16)] * 2,
        compiler_params=PARAMS,
        cost_estimate=pl.CostEstimate(flops=4 * rows * cols, bytes_accessed=8 * rows * cols, transcendentals=0),
    )(x)


def gram_kernel(scale, tile, xh_ref, xl_ref, near_ref, far_ref, kh_ref, kl_ref, ph_ref, pl_ref):
    half = near_ref.shape[0]
    ph_ref[:half], pl_ref[:half] = halves(near_ref[...])
    ph_ref[half:], pl_ref[half:] = halves(far_ref[...])
    for r in range(0, kh_ref.shape[0], tile):
        rows = slice(r, r + tile)
        xh, ph = xh_ref[rows], ph_ref[...]
        gram = mm(xh, pl_ref[...], NT) + mm(xl_ref[rows], ph, NT) + mm(xh, ph, NT)
        root = gram * scale + 0.5
        kh_ref[rows], kl_ref[rows] = halves(root * root)


def gram(x_high, x_low, near, far, tile=512):
    rows, feats = x_high.shape
    points = 2 * near.shape[0]
    return pl.pallas_call(
        lambda *refs: gram_kernel(1.0 / feats, tile, *refs),
        in_specs=[VMEM] * 4,
        out_specs=[VMEM] * 2,
        out_shape=[pltpu.VMEM((rows, points), BF16)] * 2,
        scratch_shapes=[pltpu.VMEM((points, feats), BF16)] * 2,
        compiler_params=PARAMS,
        cost_estimate=pl.CostEstimate(
            flops=6 * rows * feats * points, bytes_accessed=4 * rows * (feats + points), transcendentals=0
        ),
    )(*in_vmem(x_high, x_low), near, far)


def apply_kernel(slots, runs, tile, table_ref, *refs):
    highs, lows = refs[:slots], refs[slots:2 * slots]
    same_refs, cross_refs = refs[2 * slots:2 * slots + runs], refs[2 * slots + runs:2 * slots + 2 * runs]
    out_ref, c_ref = refs[2 * slots + 2 * runs:]
    each, half = same_refs[0].shape[:2]
    rhs = out_ref.shape[1]
    cols = pl.ds(pl.multiple_of(table_ref[slots] * rhs, rhs), rhs)
    for j in range(slots):
        place = table_ref[j]
        for i, run_refs in enumerate((same_refs, cross_refs)):
            rows = pl.ds((2 * j + i) * half, half)
            for r, ref in enumerate(run_refs):

                @pl.when((place >= r * each) & (place < (r + 1) * each))
                def _():
                    c_ref[rows, :rhs], c_ref[rows, rhs:] = halves(ref[place - r * each, :, cols])

    for r in range(0, out_ref.shape[0], tile):
        span = slice(r, r + tile)
        total = jnp.zeros((tile, rhs), F32)
        for j in range(slots):
            rows = pl.ds(2 * j * half, 2 * half)
            both = mm(highs[j][span], c_ref[rows, :], NN)
            total += both[:, :rhs] + (both[:, rhs:] + mm(lows[j][span], c_ref[rows, :rhs], NN))
        out_ref[span] = total


def apply(kerns, sames, crosses, table, parts, tile=512):
    slots, runs = len(kerns), len(sames)
    rows, points = kerns[0][0].shape
    rhs = sames[0].shape[2] // parts
    return pl.pallas_call(
        lambda *refs: apply_kernel(slots, runs, tile, *refs),
        in_specs=[pl.BlockSpec(memory_space=pltpu.SMEM)] + [VMEM] * (2 * slots + 2 * runs),
        out_specs=VMEM,
        scratch_shapes=[pltpu.VMEM((slots * points, 2 * rhs), BF16)],
        out_shape=jax.ShapeDtypeStruct((rows, rhs), F32),
        compiler_params=PARAMS,
        cost_estimate=pl.CostEstimate(
            flops=6 * rows * slots * points * rhs, bytes_accessed=4 * rows * slots * points, transcendentals=0
        ),
    )(table, *in_vmem(*[k[0] for k in kerns], *[k[1] for k in kerns]), *sames, *crosses)


def moves(depth):
    steps, held = [], {"own": {z: z for z in range(depth)}}

    def step(name, pairs, source):
        pairs = [(s, d) for s, d in pairs if s in held[source]]
        held[name] = {d: held[source][s] for s, d in pairs}
        steps.append((name, pairs, source))

    if depth == 4:
        inner, outer = [(1, 2), (2, 1)], [(1, 0), (2, 3)]
        step("a", [(0, 1), (1, 0), (2, 3), (3, 2)], "own")
        step("b", inner, "own")
        step("c", inner, "a")
        step("d", outer, "b")
        step("e", outer, "c")
    else:
        up = down = "own"
        for s in range(1, depth):
            step(f"u{s}", [(z, z + 1) for z in range(depth - 1)], up)
            step(f"d{s}", [(z, z - 1) for z in range(1, depth)], down)
            up, down = f"u{s}", f"d{s}"
    order = [name for name, _, _ in steps]
    slots = []
    for z in range(depth):
        slots.append([(name, held[name][z]) for name in order if z in held[name]])
    return steps, slots


def permute(x, pairs):
    return lax.ppermute(x, "row", pairs)


def along(pairs):
    return [(s * WIDTH + y, d * WIDTH + y) for s, d in pairs for y in range(WIDTH)]


def on_device(inverse, features, residual, block_ids):
    n = lax.axis_size("row")
    depth = n // WIDTH
    me, col = lax.axis_index("row"), lax.axis_index("col")
    cols = lax.axis_size("col")
    z, y = lax.shift_right_logical(me, 1), lax.bitwise_and(me, 1)
    across = [(r, r ^ 1) for r in range(n)]
    local_ids = block_ids - me * features.shape[0]
    half = block_ids.shape[0] // cols

    own_ids = lax.dynamic_slice_in_dim(local_ids, col * half, half)
    own = jnp.take(features, own_ids, axis=0, mode="clip")
    steps, slots = moves(depth)

    other = cols - 1 - col
    places, masks = [z], []
    for j in range(depth - 1):
        by_name, place = {}, jnp.int32(0)
        for zz in range(depth):
            by_name.setdefault(slots[zz][j][0], []).append(zz)
            place = jnp.where(z == zz, slots[zz][j][1], place)
        places.append(place)
        masks.append({name: any_of(z, zs) for name, zs in list(by_name.items())})
    ends = [(z == i) | (z == depth - 1 - i) for i in range(depth // 2 - 1)]
    tables = [jnp.stack(places + [c]).astype(jnp.int32) for c in (other, col)]
    own, local_ids, y, masks, ends, tables = lax.optimization_barrier((own, local_ids, y, masks, ends, tables))

    bufs = {"own": own}
    for name, pairs, source in steps:
        bufs[name] = permute(bufs[source], along(pairs))

    block_res = jnp.take(residual, local_ids, axis=0, mode="clip")
    partial = lax.dot_general(
        inverse.reshape(-1, inverse.shape[-1]), block_res, NN,
        precision=lax.Precision.HIGH, preferred_element_type=F32,
    ).reshape(depth, WIDTH, half, -1)
    keep = lax.dynamic_index_in_dim(partial, y, 1, keepdims=False)
    send = lax.dynamic_index_in_dim(partial, 1 - y, 1, keepdims=False)

    sames, crosses = [], []
    for h in range(2):
        run = slice(h * depth // 2, (h + 1) * depth // 2)
        term = keep[run] + permute(send[run], across)
        inward = [[(s, s + 1), (depth - 1 - s, depth - 2 - s)] for s in range(depth // 2 - 1)]
        for pairs in inward:
            term = term + permute(term, along(pairs))
        pairs = [(depth // 2 - 1, depth // 2), (depth // 2, depth // 2 - 1)]
        term = term + permute(term, along(pairs))
        for i, pairs in reversed(list(enumerate(inward))):
            back = permute(term, along([(d, s) for s, d in pairs]))
            term = jnp.where(ends[i], back, term)
        sames.append(term)
        crosses.append(permute(term, across))

    x_high, x_low = split(features)
    kerns = []
    for j in range(depth):
        block = own
        if j > 0:
            block = None
            for name, mask in masks[j - 1].items():
                block = bufs[name] if block is None else jnp.where(mask, bufs[name], block)
        far = permute(block, across)
        kerns.append(gram(x_high, x_low, block, far))

    theirs = apply(kerns, sames, crosses, tables[0], cols)
    got = lax.ppermute(theirs, "col", [(c, cols - 1 - c) for c in range(cols)])
    mine = apply(kerns, sames, crosses, tables[1], cols)
    rhs = mine.shape[1]
    return lax.dynamic_slice_in_dim(residual, col * rhs, rhs, 1) - (mine + got)


def any_of(z, places):
    mask = z == places[0]
    for p in places[1:]:
        mask = mask | (z == p)
    return mask


def solution(mesh):
    return jax.shard_map(
        on_device,
        mesh=mesh,
        in_specs=(
            P("groups", "col", None, "row"),
            P(("groups", "row"), None),
            P(("groups", "row"), None),
            P(("groups", "row")),
        ),
        out_specs=P(("groups", "row"), "col"),
        check_vma=False,
    )
```

```python
import jax
import jax.numpy as jnp
from jax import lax
from jax.experimental import pallas as pl
from jax.experimental.pallas import tpu as pltpu
from jax.sharding import PartitionSpec as P

F32, BF16 = jnp.float32, jnp.bfloat16
NT = (((1,), (1,)), ((), ()))
NN = (((1,), (0,)), ((), ()))
WIDTH = 2
RUNS = 2


def mm(a, b, dims):
    return lax.dot_general(a, b, dims, preferred_element_type=F32)


def halves(x):
    high = x.astype(BF16)
    return high, (x - high.astype(F32)).astype(BF16)


VMEM = pl.BlockSpec(memory_space=pltpu.VMEM)
PARAMS = pltpu.CompilerParams(vmem_limit_bytes=8 << 20)


def in_vmem(*arrays):
    return [pltpu.with_memory_space_constraint(a, pltpu.VMEM) for a in arrays]


def split_kernel(x_ref, high_ref, low_ref):
    high_ref[...], low_ref[...] = halves(x_ref[...])


def split(x, tile=256):
    rows, cols = x.shape
    return pl.pallas_call(
        split_kernel,
        grid=(rows // tile,),
        in_specs=[pl.BlockSpec((tile, cols), lambda i: (i, 0))],
        out_specs=[pl.BlockSpec((tile, cols), lambda i: (i, 0))] * 2,
        out_shape=[pltpu.VMEM(x.shape, BF16)] * 2,
        compiler_params=PARAMS,
        cost_estimate=pl.CostEstimate(flops=4 * rows * cols, bytes_accessed=8 * rows * cols, transcendentals=0),
    )(x)


def gather_kernel(whole, ids_ref, x_ref, out_ref, sem):
    count = out_ref.shape[0]
    first = 0 if whole else lax.axis_index("col") * count
    base = lax.axis_index("row") * x_ref.shape[0]

    @pl.loop(0, count, unroll=8)
    def _(i):
        row = ids_ref[first + i] - base
        pltpu.make_async_copy(x_ref.at[pl.ds(row, 1)], out_ref.at[pl.ds(i, 1)], sem).start()

    pltpu.make_async_copy(x_ref.at[pl.ds(0, count)], out_ref, sem).wait()


def gather(x, ids, count):
    return pl.pallas_call(
        lambda *refs: gather_kernel(count == ids.shape[0], *refs),
        in_specs=[pl.BlockSpec(memory_space=pltpu.SMEM), pl.BlockSpec(memory_space=pltpu.HBM)],
        out_specs=VMEM,
        out_shape=jax.ShapeDtypeStruct((count, x.shape[1]), x.dtype),
        scratch_shapes=[pltpu.SemaphoreType.DMA],
        compiler_params=PARAMS,
        cost_estimate=pl.CostEstimate(flops=0, bytes_accessed=8 * count * x.shape[1], transcendentals=0),
    )(ids, pltpu.with_memory_space_constraint(x, pltpu.HBM))


def partial_kernel(runs, inv_ref, res_ref, *out_refs):
    y = lax.rem(lax.axis_index("row"), WIDTH)
    high, low = halves(res_ref[...])
    for i, ref in enumerate(out_refs):
        run, side = i % runs, i // runs
        for k in range(ref.shape[0]):
            place = (run * ref.shape[0] + k) * WIDTH
            ih, il = halves(inv_ref[place + (y if side else 1 - y)])
            ref[k] = mm(ih, low, NN) + mm(il, high, NN) + mm(ih, high, NN)


def partial(inverse, res, runs):
    blocks, half, mine = inverse.shape
    shape = (blocks // WIDTH // runs, half, res.shape[1])
    outs = pl.pallas_call(
        lambda *refs: partial_kernel(runs, *refs),
        in_specs=[VMEM, VMEM],
        out_specs=[VMEM] * (2 * runs),
        out_shape=[jax.ShapeDtypeStruct(shape, F32)] * (2 * runs),
        compiler_params=PARAMS,
        cost_estimate=pl.CostEstimate(
            flops=6 * blocks * half * mine * res.shape[1], bytes_accessed=8 * blocks * half * mine, transcendentals=0
        ),
    )(inverse, res)
    return outs[:runs], outs[runs:]


def gram_kernel(scale, tile, xh_ref, xl_ref, near_ref, far_ref, kh_ref, kl_ref, ph_ref, pl_ref):
    half = near_ref.shape[0]
    ph_ref[:half], pl_ref[:half] = halves(near_ref[...])
    ph_ref[half:], pl_ref[half:] = halves(far_ref[...])
    for r in range(0, kh_ref.shape[0], tile):
        rows = slice(r, r + tile)
        xh, ph = xh_ref[rows], ph_ref[...]
        gram = mm(xh, pl_ref[...], NT) + mm(xl_ref[rows], ph, NT) + mm(xh, ph, NT)
        root = gram * scale + 0.5
        kh_ref[rows], kl_ref[rows] = halves(root * root)


def gram(x_high, x_low, near, far, tile=512):
    rows, feats = x_high.shape
    points = 2 * near.shape[0]
    return pl.pallas_call(
        lambda *refs: gram_kernel(1.0 / feats, tile, *refs),
        in_specs=[VMEM] * 4,
        out_specs=[VMEM] * 2,
        out_shape=[pltpu.VMEM((rows, points), BF16)] * 2,
        scratch_shapes=[pltpu.VMEM((points, feats), BF16)] * 2,
        compiler_params=PARAMS,
        cost_estimate=pl.CostEstimate(
            flops=6 * rows * feats * points, bytes_accessed=4 * rows * (feats + points), transcendentals=0
        ),
    )(*in_vmem(x_high, x_low), near, far)


def apply_kernel(slots, runs, tile, table_ref, *refs):
    base_ref = None
    if len(refs) > 2 * slots + 2 * runs + 2:
        base_ref, refs = refs[0], refs[1:]
    highs, lows = refs[:slots], refs[slots:2 * slots]
    same_refs, cross_refs = refs[2 * slots:2 * slots + runs], refs[2 * slots + runs:2 * slots + 2 * runs]
    out_ref, c_ref = refs[2 * slots + 2 * runs:]
    each, half = same_refs[0].shape[:2]
    rhs = out_ref.shape[1]
    cols = pl.ds(pl.multiple_of(table_ref[slots] * rhs, rhs), rhs)
    for j in range(slots):
        place = table_ref[j]
        for i, run_refs in enumerate((same_refs, cross_refs)):
            rows = pl.ds((2 * j + i) * half, half)
            for r, ref in enumerate(run_refs):

                @pl.when((place >= r * each) & (place < (r + 1) * each))
                def _():
                    c_ref[rows, :rhs], c_ref[rows, rhs:] = halves(ref[place - r * each, :, cols])

    for r in range(0, out_ref.shape[0], tile):
        span = slice(r, r + tile)
        total = jnp.zeros((tile, rhs), F32)
        for j in range(slots):
            rows = pl.ds(2 * j * half, 2 * half)
            both = mm(highs[j][span], c_ref[rows, :], NN)
            total += both[:, :rhs] + (both[:, rhs:] + mm(lows[j][span], c_ref[rows, :rhs], NN))
        out_ref[span] = total if base_ref is None else base_ref[span, cols] - total


def apply(kerns, sames, crosses, table, parts, base=(), tile=512):
    slots, runs = len(kerns), len(sames)
    rows, points = kerns[0][0].shape
    rhs = sames[0].shape[2] // parts
    return pl.pallas_call(
        lambda *refs: apply_kernel(slots, runs, tile, *refs),
        in_specs=[pl.BlockSpec(memory_space=pltpu.SMEM)] + [VMEM] * (len(base) + 2 * slots + 2 * runs),
        out_specs=VMEM,
        scratch_shapes=[pltpu.VMEM((slots * points, 2 * rhs), BF16)],
        out_shape=jax.ShapeDtypeStruct((rows, rhs), F32),
        compiler_params=PARAMS,
        cost_estimate=pl.CostEstimate(
            flops=6 * rows * slots * points * rhs, bytes_accessed=4 * rows * slots * points, transcendentals=0
        ),
    )(table, *base, *in_vmem(*[k[0] for k in kerns], *[k[1] for k in kerns]), *sames, *crosses)


def moves(depth):
    steps, held = [], {"own": {z: z for z in range(depth)}}

    def step(name, pairs, source):
        pairs = [(s, d) for s, d in pairs if s in held[source]]
        held[name] = {d: held[source][s] for s, d in pairs}
        steps.append((name, pairs, source))

    if depth == 4:
        inner, outer = [(1, 2), (2, 1)], [(1, 0), (2, 3)]
        step("a", [(0, 1), (1, 0), (2, 3), (3, 2)], "own")
        step("b", inner, "own")
        step("c", inner, "a")
        step("d", outer, "b")
        step("e", outer, "c")
    else:
        up = down = "own"
        for s in range(1, depth):
            step(f"u{s}", [(z, z + 1) for z in range(depth - 1)], up)
            step(f"d{s}", [(z, z - 1) for z in range(1, depth)], down)
            up, down = f"u{s}", f"d{s}"
    order = [name for name, _, _ in steps]
    slots = []
    for z in range(depth):
        slots.append([(name, held[name][z]) for name in order if z in held[name]])
    return steps, slots


def permute(x, pairs):
    return lax.ppermute(x, "row", pairs)


def along(pairs):
    return [(s * WIDTH + y, d * WIDTH + y) for s, d in pairs for y in range(WIDTH)]


def on_device(inverse, features, residual, block_ids):
    n = lax.axis_size("row")
    depth = n // WIDTH
    col, cols = lax.axis_index("col"), lax.axis_size("col")
    z = lax.shift_right_logical(lax.axis_index("row"), 1)
    across = [(r, r ^ 1) for r in range(n)]
    half = block_ids.shape[0] // cols

    own = gather(features, block_ids, half)
    steps, slots = moves(depth)

    other = cols - 1 - col
    places, masks = [z], []
    for j in range(depth - 1):
        by_name, place = {}, jnp.int32(0)
        for zz in range(depth):
            by_name.setdefault(slots[zz][j][0], []).append(zz)
            place = jnp.where(z == zz, slots[zz][j][1], place)
        places.append(place)
        masks.append({name: any_of(z, zs) for name, zs in list(by_name.items())})
    ends = [(z == i) | (z == depth - 1 - i) for i in range(depth // 2 - 1)]
    tables = [jnp.stack(places + [c]).astype(jnp.int32) for c in (other, col)]
    own, masks, ends, tables = lax.optimization_barrier((own, masks, ends, tables))

    bufs = {"own": own}
    for name, pairs, source in steps:
        bufs[name] = permute(bufs[source], along(pairs))

    res = gather(residual, block_ids, block_ids.shape[0])
    send, keep = partial(inverse.reshape(n, half, -1), res, RUNS)

    sames, crosses = [], []
    for h in range(RUNS):
        term = keep[h] + permute(send[h], across)
        inward = [[(s, s + 1), (depth - 1 - s, depth - 2 - s)] for s in range(depth // 2 - 1)]
        for pairs in inward:
            term = term + permute(term, along(pairs))
        pairs = [(depth // 2 - 1, depth // 2), (depth // 2, depth // 2 - 1)]
        term = term + permute(term, along(pairs))
        for i, pairs in reversed(list(enumerate(inward))):
            back = permute(term, along([(d, s) for s, d in pairs]))
            term = jnp.where(ends[i], back, term)
        sames.append(term)
        crosses.append(permute(term, across))

    x_high, x_low = split(features)
    kerns = []
    for j in range(depth):
        block = own
        if j > 0:
            block = None
            for name, mask in masks[j - 1].items():
                block = bufs[name] if block is None else jnp.where(mask, bufs[name], block)
        far = permute(block, across)
        kerns.append(gram(x_high, x_low, block, far))

    theirs = apply(kerns, sames, crosses, tables[0], cols)
    got = lax.ppermute(theirs, "col", [(c, cols - 1 - c) for c in range(cols)])
    mine = apply(kerns, sames, crosses, tables[1], cols, (residual,))
    return mine - got


def any_of(z, places):
    mask = z == places[0]
    for p in places[1:]:
        mask = mask | (z == p)
    return mask


def solution(mesh):
    return jax.shard_map(
        on_device,
        mesh=mesh,
        in_specs=(
            P("groups", "col", None, "row"),
            P(("groups", "row"), None),
            P(("groups", "row"), None),
            P(("groups", "row")),
        ),
        out_specs=P(("groups", "row"), "col"),
        check_vma=False,
    )
```

```python
import jax
import jax.numpy as jnp
from jax import lax
from jax.experimental import pallas as pl
from jax.experimental.pallas import tpu as pltpu
from jax.sharding import PartitionSpec as P

F32, BF16 = jnp.float32, jnp.bfloat16
NT = (((1,), (1,)), ((), ()))
NN = (((1,), (0,)), ((), ()))
WIDTH = 2
RUNS = 2


def mm(a, b, dims):
    return lax.dot_general(a, b, dims, preferred_element_type=F32)


def halves(x):
    high = x.astype(BF16)
    return high, (x - high.astype(F32)).astype(BF16)


VMEM = pl.BlockSpec(memory_space=pltpu.VMEM)
PARAMS = pltpu.CompilerParams(vmem_limit_bytes=8 << 20)


def in_vmem(*arrays):
    return [pltpu.with_memory_space_constraint(a, pltpu.VMEM) for a in arrays]


def split_kernel(x_ref, high_ref, low_ref):
    high_ref[...], low_ref[...] = halves(x_ref[...])


def split(x, tile=256):
    rows, cols = x.shape
    return pl.pallas_call(
        split_kernel,
        grid=(rows // tile,),
        in_specs=[pl.BlockSpec((tile, cols), lambda i: (i, 0))],
        out_specs=[pl.BlockSpec((tile, cols), lambda i: (i, 0))] * 2,
        out_shape=[pltpu.VMEM(x.shape, BF16)] * 2,
        compiler_params=PARAMS,
        cost_estimate=pl.CostEstimate(flops=4 * rows * cols, bytes_accessed=8 * rows * cols, transcendentals=0),
    )(x)


def gather_kernel(whole, ids_hbm, x_ref, out_ref, ids_ref, ids_sem, sem):
    copy = pltpu.make_async_copy(ids_hbm, ids_ref, ids_sem)
    copy.start()
    copy.wait()
    count = out_ref.shape[0]
    first = 0 if whole else lax.axis_index("col") * count
    base = lax.axis_index("row") * x_ref.shape[0]

    @pl.loop(0, count, unroll=8)
    def _(i):
        row = ids_ref[first + i] - base
        pltpu.make_async_copy(x_ref.at[pl.ds(row, 1)], out_ref.at[pl.ds(i, 1)], sem).start()

    pltpu.make_async_copy(x_ref.at[pl.ds(0, count)], out_ref, sem).wait()


def gather(x, ids, count):
    return pl.pallas_call(
        lambda *refs: gather_kernel(count == ids.shape[0], *refs),
        in_specs=[pl.BlockSpec(memory_space=pltpu.HBM)] * 2,
        out_specs=VMEM,
        out_shape=jax.ShapeDtypeStruct((count, x.shape[1]), x.dtype),
        scratch_shapes=[pltpu.SMEM(ids.shape, ids.dtype), pltpu.SemaphoreType.DMA, pltpu.SemaphoreType.DMA],
        compiler_params=PARAMS,
        cost_estimate=pl.CostEstimate(flops=0, bytes_accessed=8 * count * x.shape[1], transcendentals=0),
    )(*[pltpu.with_memory_space_constraint(a, pltpu.HBM) for a in (ids, x)])


def partial_kernel(runs, inv_ref, res_ref, *out_refs):
    y = lax.rem(lax.axis_index("row"), WIDTH)
    high, low = halves(res_ref[...])
    for i, ref in enumerate(out_refs):
        run, side = i % runs, i // runs
        for k in range(ref.shape[0]):
            place = (run * ref.shape[0] + k) * WIDTH
            ih, il = halves(inv_ref[place + (y if side else 1 - y)])
            ref[k] = mm(ih, low, NN) + mm(il, high, NN) + mm(ih, high, NN)


def partial(inverse, res, runs):
    blocks, half, mine = inverse.shape
    shape = (blocks // WIDTH // runs, half, res.shape[1])
    outs = pl.pallas_call(
        lambda *refs: partial_kernel(runs, *refs),
        in_specs=[VMEM, VMEM],
        out_specs=[VMEM] * (2 * runs),
        out_shape=[jax.ShapeDtypeStruct(shape, F32)] * (2 * runs),
        compiler_params=PARAMS,
        cost_estimate=pl.CostEstimate(
            flops=6 * blocks * half * mine * res.shape[1], bytes_accessed=8 * blocks * half * mine, transcendentals=0
        ),
    )(inverse, res)
    return outs[:runs], outs[runs:]


def gram_kernel(scale, tile, xh_ref, xl_ref, near_ref, far_ref, kh_ref, kl_ref, ph_ref, pl_ref):
    half = near_ref.shape[0]
    ph_ref[:half], pl_ref[:half] = halves(near_ref[...])
    ph_ref[half:], pl_ref[half:] = halves(far_ref[...])
    for r in range(0, kh_ref.shape[0], tile):
        rows = slice(r, r + tile)
        xh, ph = xh_ref[rows], ph_ref[...]
        gram = mm(xh, pl_ref[...], NT) + mm(xl_ref[rows], ph, NT) + mm(xh, ph, NT)
        root = gram * scale + 0.5
        kh_ref[rows], kl_ref[rows] = halves(root * root)


def gram(x_high, x_low, near, far, tile=512):
    rows, feats = x_high.shape
    points = 2 * near.shape[0]
    return pl.pallas_call(
        lambda *refs: gram_kernel(1.0 / feats, tile, *refs),
        in_specs=[VMEM] * 4,
        out_specs=[VMEM] * 2,
        out_shape=[pltpu.VMEM((rows, points), BF16)] * 2,
        scratch_shapes=[pltpu.VMEM((points, feats), BF16)] * 2,
        compiler_params=PARAMS,
        cost_estimate=pl.CostEstimate(
            flops=6 * rows * feats * points, bytes_accessed=4 * rows * (feats + points), transcendentals=0
        ),
    )(*in_vmem(x_high, x_low), near, far)


def apply_kernel(slots, runs, tile, table_ref, *refs):
    base_ref = None
    if len(refs) > 2 * slots + 2 * runs + 2:
        base_ref, refs = refs[0], refs[1:]
    highs, lows = refs[:slots], refs[slots:2 * slots]
    same_refs, cross_refs = refs[2 * slots:2 * slots + runs], refs[2 * slots + runs:2 * slots + 2 * runs]
    out_ref, c_ref = refs[2 * slots + 2 * runs:]
    each, half = same_refs[0].shape[:2]
    rhs = out_ref.shape[1]
    cols = pl.ds(pl.multiple_of(table_ref[slots] * rhs, rhs), rhs)
    for j in range(slots):
        place = table_ref[j]
        for i, run_refs in enumerate((same_refs, cross_refs)):
            rows = pl.ds((2 * j + i) * half, half)
            for r, ref in enumerate(run_refs):

                @pl.when((place >= r * each) & (place < (r + 1) * each))
                def _():
                    c_ref[rows, :rhs], c_ref[rows, rhs:] = halves(ref[place - r * each, :, cols])

    for r in range(0, out_ref.shape[0], tile):
        span = slice(r, r + tile)
        high = jnp.concatenate([ref[span] for ref in highs], 1)
        low = jnp.concatenate([ref[span] for ref in lows], 1)
        both = mm(high, c_ref[...], NN)
        total = both[:, :rhs] + (both[:, rhs:] + mm(low, c_ref[:, :rhs], NN))
        out_ref[span] = total if base_ref is None else base_ref[span, cols] - total


def apply(kerns, sames, crosses, table, parts, base=(), tile=512):
    slots, runs = len(kerns), len(sames)
    rows, points = kerns[0][0].shape
    rhs = sames[0].shape[2] // parts
    return pl.pallas_call(
        lambda *refs: apply_kernel(slots, runs, tile, *refs),
        in_specs=[pl.BlockSpec(memory_space=pltpu.SMEM)] + [VMEM] * (len(base) + 2 * slots + 2 * runs),
        out_specs=VMEM,
        scratch_shapes=[pltpu.VMEM((slots * points, 2 * rhs), BF16)],
        out_shape=jax.ShapeDtypeStruct((rows, rhs), F32),
        compiler_params=PARAMS,
        cost_estimate=pl.CostEstimate(
            flops=6 * rows * slots * points * rhs, bytes_accessed=4 * rows * slots * points, transcendentals=0
        ),
    )(table, *base, *in_vmem(*[k[0] for k in kerns], *[k[1] for k in kerns]), *sames, *crosses)


def moves(depth):
    steps, held = [], {"own": {z: z for z in range(depth)}}

    def step(name, pairs, source):
        pairs = [(s, d) for s, d in pairs if s in held[source]]
        held[name] = {d: held[source][s] for s, d in pairs}
        steps.append((name, pairs, source))

    if depth == 4:
        inner, outer = [(1, 2), (2, 1)], [(1, 0), (2, 3)]
        step("a", [(0, 1), (1, 0), (2, 3), (3, 2)], "own")
        step("b", inner, "own")
        step("c", inner, "a")
        step("d", outer, "b")
        step("e", outer, "c")
    else:
        up = down = "own"
        for s in range(1, depth):
            step(f"u{s}", [(z, z + 1) for z in range(depth - 1)], up)
            step(f"d{s}", [(z, z - 1) for z in range(1, depth)], down)
            up, down = f"u{s}", f"d{s}"
    order = [name for name, _, _ in steps]
    slots = []
    for z in range(depth):
        slots.append([(name, held[name][z]) for name in order if z in held[name]])
    return steps, slots


def permute(x, pairs):
    return lax.ppermute(x, "row", pairs)


def along(pairs):
    return [(s * WIDTH + y, d * WIDTH + y) for s, d in pairs for y in range(WIDTH)]


def on_device(inverse, features, residual, block_ids):
    n = lax.axis_size("row")
    depth = n // WIDTH
    col, cols = lax.axis_index("col"), lax.axis_size("col")
    z = lax.shift_right_logical(lax.axis_index("row"), 1)
    across = [(r, r ^ 1) for r in range(n)]
    half = block_ids.shape[0] // cols

    own = gather(features, block_ids, half)
    steps, slots = moves(depth)

    other = cols - 1 - col
    places, masks = [z], []
    for j in range(depth - 1):
        by_name, place = {}, jnp.int32(0)
        for zz in range(depth):
            by_name.setdefault(slots[zz][j][0], []).append(zz)
            place = jnp.where(z == zz, slots[zz][j][1], place)
        places.append(place)
        masks.append({name: any_of(z, zs) for name, zs in list(by_name.items())})
    ends = [(z == i) | (z == depth - 1 - i) for i in range(depth // 2 - 1)]
    tables = [jnp.stack(places + [c]).astype(jnp.int32) for c in (other, col)]
    own, masks, ends, tables = lax.optimization_barrier((own, masks, ends, tables))

    bufs = {"own": own}
    for name, pairs, source in steps:
        bufs[name] = permute(bufs[source], along(pairs))

    res = gather(residual, block_ids, block_ids.shape[0])
    send, keep = partial(inverse.reshape(n, half, -1), res, RUNS)

    sames, crosses = [], []
    for h in range(RUNS):
        term = keep[h] + permute(send[h], across)
        inward = [[(s, s + 1), (depth - 1 - s, depth - 2 - s)] for s in range(depth // 2 - 1)]
        for pairs in inward:
            term = term + permute(term, along(pairs))
        pairs = [(depth // 2 - 1, depth // 2), (depth // 2, depth // 2 - 1)]
        term = term + permute(term, along(pairs))
        for i, pairs in reversed(list(enumerate(inward))):
            back = permute(term, along([(d, s) for s, d in pairs]))
            term = jnp.where(ends[i], back, term)
        sames.append(term)
        crosses.append(permute(term, across))

    x_high, x_low = split(features)
    kerns, fars = [], []
    for j in range(depth):
        block = own
        if j > 0:
            block = None
            for name, mask in masks[j - 1].items():
                block = bufs[name] if block is None else jnp.where(mask, bufs[name], block)
        if j == 1 and depth == 4:
            far = permute(fars[0], along(steps[0][1]))
        else:
            far = permute(block, across)
        fars.append(far)
        kerns.append(gram(x_high, x_low, block, far))

    theirs = apply(kerns, sames, crosses, tables[0], cols)
    got = lax.ppermute(theirs, "col", [(c, cols - 1 - c) for c in range(cols)])
    mine = apply(kerns, sames, crosses, tables[1], cols, (residual,))
    return mine - got


def any_of(z, places):
    mask = z == places[0]
    for p in places[1:]:
        mask = mask | (z == p)
    return mask


def solution(mesh):
    return jax.shard_map(
        on_device,
        mesh=mesh,
        in_specs=(
            P("groups", "col", None, "row"),
            P(("groups", "row"), None),
            P(("groups", "row"), None),
            P(("groups", "row")),
        ),
        out_specs=P(("groups", "row"), "col"),
        check_vma=False,
    )
```

```python
import jax
import jax.numpy as jnp
from jax import lax
from jax.experimental import pallas as pl
from jax.experimental.pallas import tpu as pltpu
from jax.sharding import PartitionSpec as P

F32, BF16 = jnp.float32, jnp.bfloat16
NT = (((1,), (1,)), ((), ()))
NN = (((1,), (0,)), ((), ()))
WIDTH = 2
RUNS = 2


def mm(a, b, dims):
    return lax.dot_general(a, b, dims, preferred_element_type=F32)


def halves(x):
    high = x.astype(BF16)
    return high, (x - high.astype(F32)).astype(BF16)


VMEM = pl.BlockSpec(memory_space=pltpu.VMEM)
PARAMS = pltpu.CompilerParams(vmem_limit_bytes=8 << 20)


def in_vmem(*arrays):
    return [pltpu.with_memory_space_constraint(a, pltpu.VMEM) for a in arrays]


def split_kernel(x_ref, high_ref, low_ref):
    high_ref[...], low_ref[...] = halves(x_ref[...])


def split(x, tile=256):
    rows, cols = x.shape
    return pl.pallas_call(
        split_kernel,
        grid=(rows // tile,),
        in_specs=[pl.BlockSpec((tile, cols), lambda i: (i, 0))],
        out_specs=[pl.BlockSpec((tile, cols), lambda i: (i, 0))] * 2,
        out_shape=[pltpu.VMEM(x.shape, BF16)] * 2,
        compiler_params=PARAMS,
        cost_estimate=pl.CostEstimate(flops=4 * rows * cols, bytes_accessed=8 * rows * cols, transcendentals=0),
    )(x)


def gather_kernel(whole, ids_hbm, x_ref, out_ref, ids_ref, ids_sem, sem):
    copy = pltpu.make_async_copy(ids_hbm, ids_ref, ids_sem)
    copy.start()
    copy.wait()
    count = out_ref.shape[0]
    first = 0 if whole else lax.axis_index("col") * count
    base = lax.axis_index("row") * x_ref.shape[0]

    @pl.loop(0, count, unroll=8)
    def _(i):
        row = ids_ref[first + i] - base
        pltpu.make_async_copy(x_ref.at[pl.ds(row, 1)], out_ref.at[pl.ds(i, 1)], sem).start()

    pltpu.make_async_copy(x_ref.at[pl.ds(0, count)], out_ref, sem).wait()


def gather(x, ids, count):
    return pl.pallas_call(
        lambda *refs: gather_kernel(count == ids.shape[0], *refs),
        in_specs=[pl.BlockSpec(memory_space=pltpu.HBM)] * 2,
        out_specs=VMEM,
        out_shape=jax.ShapeDtypeStruct((count, x.shape[1]), x.dtype),
        scratch_shapes=[pltpu.SMEM(ids.shape, ids.dtype), pltpu.SemaphoreType.DMA, pltpu.SemaphoreType.DMA],
        compiler_params=PARAMS,
        cost_estimate=pl.CostEstimate(flops=0, bytes_accessed=8 * count * x.shape[1], transcendentals=0),
    )(*[pltpu.with_memory_space_constraint(a, pltpu.HBM) for a in (ids, x)])


def partial_kernel(runs, inv_ref, res_ref, *out_refs):
    y = lax.rem(lax.axis_index("row"), WIDTH)
    high, low = halves(res_ref[...])
    for i, ref in enumerate(out_refs):
        run, side = i % runs, i // runs
        for k in range(ref.shape[0]):
            place = (run * ref.shape[0] + k) * WIDTH
            ih, il = halves(inv_ref[place + (y if side else 1 - y)])
            ref[k] = mm(ih, low, NN) + mm(il, high, NN) + mm(ih, high, NN)


def partial(inverse, res, runs):
    blocks, half, mine = inverse.shape
    shape = (blocks // WIDTH // runs, half, res.shape[1])
    outs = pl.pallas_call(
        lambda *refs: partial_kernel(runs, *refs),
        in_specs=[VMEM, VMEM],
        out_specs=[VMEM] * (2 * runs),
        out_shape=[jax.ShapeDtypeStruct(shape, F32)] * (2 * runs),
        compiler_params=PARAMS,
        cost_estimate=pl.CostEstimate(
            flops=6 * blocks * half * mine * res.shape[1], bytes_accessed=8 * blocks * half * mine, transcendentals=0
        ),
    )(inverse, res)
    return outs[:runs], outs[runs:]


def gram_kernel(scale, tile, xh_ref, xl_ref, near_ref, far_ref, kh_ref, kl_ref, ph_ref, pl_ref):
    half = near_ref.shape[0]
    ph_ref[:half], pl_ref[:half] = halves(near_ref[...])
    ph_ref[half:], pl_ref[half:] = halves(far_ref[...])
    for r in range(0, kh_ref.shape[0], tile):
        rows = slice(r, r + tile)
        xh, ph = xh_ref[rows], ph_ref[...]
        gram = mm(xh, pl_ref[...], NT) + mm(xl_ref[rows], ph, NT) + mm(xh, ph, NT)
        root = gram * scale + 0.5
        kh_ref[rows], kl_ref[rows] = halves(root * root)


def gram(x_high, x_low, near, far, tile=512):
    rows, feats = x_high.shape
    points = 2 * near.shape[0]
    return pl.pallas_call(
        lambda *refs: gram_kernel(1.0 / feats, tile, *refs),
        in_specs=[VMEM] * 4,
        out_specs=[VMEM] * 2,
        out_shape=[pltpu.VMEM((rows, points), BF16)] * 2,
        scratch_shapes=[pltpu.VMEM((points, feats), BF16)] * 2,
        compiler_params=PARAMS,
        cost_estimate=pl.CostEstimate(
            flops=6 * rows * feats * points, bytes_accessed=4 * rows * (feats + points), transcendentals=0
        ),
    )(*in_vmem(x_high, x_low), near, far)


def fill(c_ref, row, ref, place, cols):
    half, rhs = ref.shape[1], c_ref.shape[1] // 2 // len(cols)
    rows = pl.ds(row, half)
    for i, col in enumerate(cols):
        span = pl.ds(pl.multiple_of(col * rhs, rhs), rhs)
        high, low = halves(ref[place, :, span])
        c_ref[rows, i * rhs:(i + 1) * rhs] = high
        c_ref[rows, (len(cols) + i) * rhs:(len(cols) + i + 1) * rhs] = low


def product(kerns, slots, places, run_refs, cols, c_ref, tile, store):
    each, half = run_refs[0].shape[:2]
    for i, slot in enumerate(slots):
        place = places[slot]
        for r, ref in enumerate(run_refs):

            @pl.when((place >= r * each) & (place < (r + 1) * each))
            def _():
                fill(c_ref, i * half, ref, place - r * each, cols)

    width = c_ref.shape[1] // 2
    for r in range(0, kerns[0].shape[0], tile):
        span = slice(r, r + tile)
        high = jnp.concatenate([ref[span] for ref in kerns[::2]], 1)
        low = jnp.concatenate([ref[span] for ref in kerns[1::2]], 1)
        both = mm(high, c_ref[...], NN)
        store(span, both[:, :width] + (both[:, width:] + mm(low, c_ref[:, :width], NN)))


def call(kernel, kerns, runs, others, table, outs, scratch, cost):
    return pl.pallas_call(
        kernel,
        in_specs=[pl.BlockSpec(memory_space=pltpu.SMEM)] + [VMEM] * (len(kerns) + len(runs) + len(others)),
        out_specs=[VMEM] * outs[0],
        out_shape=[pltpu.VMEM(outs[1], F32)] * outs[0],
        scratch_shapes=[pltpu.VMEM(scratch, BF16)],
        compiler_params=PARAMS,
        cost_estimate=pl.CostEstimate(flops=cost, bytes_accessed=cost // 1024, transcendentals=0),
    )(table, *in_vmem(*kerns), *runs, *in_vmem(*others))


def apply_near(kerns, slots, runs, table, residual, parts, tile=512):
    rows, count = kerns[0].shape[0], len(kerns)
    half, rhs = runs[0].shape[1], runs[0].shape[2] // parts

    def kernel(table_ref, *refs):
        base_ref, theirs_ref, mine_ref, c_ref = refs[count + len(runs):]
        col = table_ref[len(slots)]
        span = pl.ds(pl.multiple_of(col * rhs, rhs), rhs)

        def store(at, value):
            theirs_ref[at] = value[:, :rhs]
            mine_ref[at] = base_ref[at, span] - value[:, rhs:]

        product(refs[:count], slots, table_ref, refs[count:count + len(runs)], (parts - 1 - col, col), c_ref, tile, store)

    scratch = (len(slots) * half, 4 * rhs)
    return call(
        kernel, kerns, runs, [residual], table, (2, (rows, rhs)), scratch, 6 * rows * scratch[0] * 2 * rhs
    )


def apply_far(kerns, slots, runs, table, base, mine, parts, tile=512):
    rows, count = kerns[0].shape[0], len(kerns)
    half, rhs = runs[0].shape[1], runs[0].shape[2] // parts

    def kernel(table_ref, *refs):
        base_ref, out_ref, c_ref = refs[count + len(runs):]
        col = table_ref[len(slots)]

        def store(at, value):
            out_ref[at] = base_ref[at] - value if mine else base_ref[at] + value

        cols = (col if mine else parts - 1 - col,)
        product(refs[:count], slots, table_ref, refs[count:count + len(runs)], cols, c_ref, tile, store)

    scratch = (len(slots) * half, 2 * rhs)
    return call(kernel, kerns, runs, [base], table, (1, (rows, rhs)), scratch, 6 * rows * scratch[0] * rhs)[0]


def moves(depth):
    steps, held = [], {"own": {z: z for z in range(depth)}}

    def step(name, pairs, source):
        pairs = [(s, d) for s, d in pairs if s in held[source]]
        held[name] = {d: held[source][s] for s, d in pairs}
        steps.append((name, pairs, source))

    if depth == 4:
        inner, outer = [(1, 2), (2, 1)], [(1, 0), (2, 3)]
        step("a", [(0, 1), (1, 0), (2, 3), (3, 2)], "own")
        step("b", inner, "own")
        step("c", inner, "a")
        step("d", outer, "b")
        step("e", outer, "c")
    else:
        up = down = "own"
        for s in range(1, depth):
            step(f"u{s}", [(z, z + 1) for z in range(depth - 1)], up)
            step(f"d{s}", [(z, z - 1) for z in range(1, depth)], down)
            up, down = f"u{s}", f"d{s}"
    order = [name for name, _, _ in steps]
    slots = []
    for z in range(depth):
        slots.append([(name, held[name][z]) for name in order if z in held[name]])
    return steps, slots


def permute(x, pairs):
    return lax.ppermute(x, "row", pairs)


def along(pairs):
    return [(s * WIDTH + y, d * WIDTH + y) for s, d in pairs for y in range(WIDTH)]


def on_device(inverse, features, residual, block_ids):
    n = lax.axis_size("row")
    depth = n // WIDTH
    col, cols = lax.axis_index("col"), lax.axis_size("col")
    z = lax.shift_right_logical(lax.axis_index("row"), 1)
    across = [(r, r ^ 1) for r in range(n)]
    half = block_ids.shape[0] // cols

    own = gather(features, block_ids, half)
    steps, slots = moves(depth)

    places, masks = [z], []
    for j in range(depth - 1):
        by_name, place = {}, jnp.int32(0)
        for zz in range(depth):
            by_name.setdefault(slots[zz][j][0], []).append(zz)
            place = jnp.where(z == zz, slots[zz][j][1], place)
        places.append(place)
        masks.append({name: any_of(z, zs) for name, zs in list(by_name.items())})
    ends = [(z == i) | (z == depth - 1 - i) for i in range(depth // 2 - 1)]
    table = jnp.stack(places + [col]).astype(jnp.int32)
    own, masks, ends, table = lax.optimization_barrier((own, masks, ends, table))

    bufs = {"own": own}
    for name, pairs, source in steps:
        bufs[name] = permute(bufs[source], along(pairs))

    res = gather(residual, block_ids, block_ids.shape[0])
    send, keep = partial(inverse.reshape(n, half, -1), res, RUNS)

    sames, crosses = [], []
    for h in range(RUNS):
        term = keep[h] + permute(send[h], across)
        inward = [[(s, s + 1), (depth - 1 - s, depth - 2 - s)] for s in range(depth // 2 - 1)]
        for pairs in inward:
            term = term + permute(term, along(pairs))
        pairs = [(depth // 2 - 1, depth // 2), (depth // 2, depth // 2 - 1)]
        term = term + permute(term, along(pairs))
        for i, pairs in reversed(list(enumerate(inward))):
            back = permute(term, along([(d, s) for s, d in pairs]))
            term = jnp.where(ends[i], back, term)
        sames.append(term)
        crosses.append(permute(term, across))

    x_high, x_low = split(features)
    nears, fars = [], []
    for j in range(depth):
        block = own
        if j > 0:
            block = None
            for name, mask in masks[j - 1].items():
                block = bufs[name] if block is None else jnp.where(mask, bufs[name], block)
        nears.append(block)
        if j == 1 and depth == 4:
            fars.append(permute(fars[0], along(steps[0][1])))
        else:
            fars.append(permute(block, across))
    near_slots = list(range(depth))
    far_slots = [0, 2, 1, 3] if depth == 4 else near_slots
    near_kerns, far_kerns = [], []
    for i in range(0, depth, 2):
        near_kerns += gram(x_high, x_low, *[nears[j] for j in near_slots[i:i + 2]])
        far_kerns += gram(x_high, x_low, *[fars[j] for j in far_slots[i:i + 2]])

    theirs, mine = apply_near(near_kerns, near_slots, sames, table, residual, cols)
    theirs = apply_far(far_kerns, far_slots, crosses, table, theirs, False, cols)
    got = lax.ppermute(theirs, "col", [(c, cols - 1 - c) for c in range(cols)])
    mine = apply_far(far_kerns, far_slots, crosses, table, mine, True, cols)
    return mine - got


def any_of(z, places):
    mask = z == places[0]
    for p in places[1:]:
        mask = mask | (z == p)
    return mask


def solution(mesh):
    return jax.shard_map(
        on_device,
        mesh=mesh,
        in_specs=(
            P("groups", "col", None, "row"),
            P(("groups", "row"), None),
            P(("groups", "row"), None),
            P(("groups", "row")),
        ),
        out_specs=P(("groups", "row"), "col"),
        check_vma=False,
    )
```

```python
import jax
import jax.numpy as jnp
from jax import lax
from jax.experimental import pallas as pl
from jax.experimental.pallas import tpu as pltpu
from jax.sharding import PartitionSpec as P

F32, BF16 = jnp.float32, jnp.bfloat16
NT = (((1,), (1,)), ((), ()))
NN = (((1,), (0,)), ((), ()))
WIDTH = 2
RUNS = 2


def mm(a, b, dims):
    return lax.dot_general(a, b, dims, preferred_element_type=F32)


def halves(x):
    high = x.astype(BF16)
    return high, (x - high.astype(F32)).astype(BF16)


VMEM = pl.BlockSpec(memory_space=pltpu.VMEM)
PARAMS = pltpu.CompilerParams(vmem_limit_bytes=8 << 20)


def in_vmem(*arrays):
    return [pltpu.with_memory_space_constraint(a, pltpu.VMEM) for a in arrays]


def split_kernel(x_ref, high_ref, low_ref):
    high_ref[...], low_ref[...] = halves(x_ref[...])


def split(x, tile=256):
    rows, cols = x.shape
    return pl.pallas_call(
        split_kernel,
        grid=(rows // tile,),
        in_specs=[pl.BlockSpec((tile, cols), lambda i: (i, 0))],
        out_specs=[pl.BlockSpec((tile, cols), lambda i: (i, 0))] * 2,
        out_shape=[pltpu.VMEM(x.shape, BF16)] * 2,
        compiler_params=PARAMS,
        cost_estimate=pl.CostEstimate(flops=4 * rows * cols, bytes_accessed=8 * rows * cols, transcendentals=0),
    )(x)


def gather_kernel(whole, ids_hbm, x_ref, out_ref, ids_ref, ids_sem, sem):
    copy = pltpu.make_async_copy(ids_hbm, ids_ref, ids_sem)
    copy.start()
    copy.wait()
    count = out_ref.shape[0]
    first = 0 if whole else lax.axis_index("col") * count
    base = lax.axis_index("row") * x_ref.shape[0]

    @pl.loop(0, count, unroll=8)
    def _(i):
        row = ids_ref[first + i] - base
        pltpu.make_async_copy(x_ref.at[pl.ds(row, 1)], out_ref.at[pl.ds(i, 1)], sem).start()

    pltpu.make_async_copy(x_ref.at[pl.ds(0, count)], out_ref, sem).wait()


def gather(x, ids, count):
    return pl.pallas_call(
        lambda *refs: gather_kernel(count == ids.shape[0], *refs),
        in_specs=[pl.BlockSpec(memory_space=pltpu.HBM)] * 2,
        out_specs=VMEM,
        out_shape=jax.ShapeDtypeStruct((count, x.shape[1]), x.dtype),
        scratch_shapes=[pltpu.SMEM(ids.shape, ids.dtype), pltpu.SemaphoreType.DMA, pltpu.SemaphoreType.DMA],
        compiler_params=PARAMS,
        cost_estimate=pl.CostEstimate(flops=0, bytes_accessed=8 * count * x.shape[1], transcendentals=0),
    )(*[pltpu.with_memory_space_constraint(a, pltpu.HBM) for a in (ids, x)])


def partial_kernel(runs, inv_ref, res_ref, *out_refs):
    y = lax.rem(lax.axis_index("row"), WIDTH)
    high, low = halves(res_ref[...])
    for i, ref in enumerate(out_refs):
        run, side = i % runs, i // runs
        for k in range(ref.shape[0]):
            place = (run * ref.shape[0] + k) * WIDTH
            ih, il = halves(inv_ref[place + (y if side else 1 - y)])
            ref[k] = mm(ih, low, NN) + mm(il, high, NN) + mm(ih, high, NN)


def partial(inverse, res, runs):
    blocks, half, mine = inverse.shape
    shape = (blocks // WIDTH // runs, half, res.shape[1])
    outs = pl.pallas_call(
        lambda *refs: partial_kernel(runs, *refs),
        in_specs=[VMEM, VMEM],
        out_specs=[VMEM] * (2 * runs),
        out_shape=[jax.ShapeDtypeStruct(shape, F32)] * (2 * runs),
        compiler_params=PARAMS,
        cost_estimate=pl.CostEstimate(
            flops=6 * blocks * half * mine * res.shape[1], bytes_accessed=8 * blocks * half * mine, transcendentals=0
        ),
    )(inverse, res)
    return outs[:runs], outs[runs:]


def gram_kernel(scale, tile, xh_ref, xl_ref, near_ref, far_ref, kh_ref, kl_ref, ph_ref, pl_ref):
    half = near_ref.shape[0]
    ph_ref[:half], pl_ref[:half] = halves(near_ref[...])
    ph_ref[half:], pl_ref[half:] = halves(far_ref[...])
    for r in range(0, kh_ref.shape[0], tile):
        rows = slice(r, r + tile)
        xh, ph = xh_ref[rows], ph_ref[...]
        gram = mm(xh, pl_ref[...], NT) + mm(xl_ref[rows], ph, NT) + mm(xh, ph, NT)
        root = gram * scale + 0.5
        kh_ref[rows], kl_ref[rows] = halves(root * root)


def gram(x_high, x_low, near, far, tile=1024):
    rows, feats = x_high.shape
    points = 2 * near.shape[0]
    return pl.pallas_call(
        lambda *refs: gram_kernel(1.0 / feats, tile, *refs),
        in_specs=[VMEM] * 4,
        out_specs=[VMEM] * 2,
        out_shape=[pltpu.VMEM((rows, points), BF16)] * 2,
        scratch_shapes=[pltpu.VMEM((points, feats), BF16)] * 2,
        compiler_params=PARAMS,
        cost_estimate=pl.CostEstimate(
            flops=6 * rows * feats * points, bytes_accessed=4 * rows * (feats + points), transcendentals=0
        ),
    )(*in_vmem(x_high, x_low), near, far)


def fill(c_ref, row, ref, place, cols):
    half, rhs = ref.shape[1], c_ref.shape[1] // 2 // len(cols)
    rows = pl.ds(row, half)
    for i, col in enumerate(cols):
        span = pl.ds(pl.multiple_of(col * rhs, rhs), rhs)
        high, low = halves(ref[place, :, span])
        c_ref[rows, i * rhs:(i + 1) * rhs] = high
        c_ref[rows, (len(cols) + i) * rhs:(len(cols) + i + 1) * rhs] = low


def product(kerns, slots, places, run_refs, cols, c_ref, tile, store):
    each, half = run_refs[0].shape[:2]
    for i, slot in enumerate(slots):
        place = places[slot]
        for r, ref in enumerate(run_refs):

            @pl.when((place >= r * each) & (place < (r + 1) * each))
            def _():
                fill(c_ref, i * half, ref, place - r * each, cols)

    width = c_ref.shape[1] // 2
    for r in range(0, kerns[0].shape[0], tile):
        span = slice(r, r + tile)
        high = jnp.concatenate([ref[span] for ref in kerns[::2]], 1)
        low = jnp.concatenate([ref[span] for ref in kerns[1::2]], 1)
        both = mm(high, c_ref[...], NN)
        store(span, both[:, :width] + (both[:, width:] + mm(low, c_ref[:, :width], NN)))


def call(kernel, kerns, runs, others, table, outs, scratch, cost):
    return pl.pallas_call(
        kernel,
        in_specs=[pl.BlockSpec(memory_space=pltpu.SMEM)] + [VMEM] * (len(kerns) + len(runs) + len(others)),
        out_specs=[VMEM] * outs[0],
        out_shape=[pltpu.VMEM(outs[1], F32)] * outs[0],
        scratch_shapes=[pltpu.VMEM(scratch, BF16)],
        compiler_params=PARAMS,
        cost_estimate=pl.CostEstimate(flops=cost, bytes_accessed=cost // 1024, transcendentals=0),
    )(table, *in_vmem(*kerns), *runs, *in_vmem(*others))


def apply_near(kerns, slots, runs, table, residual, parts, tile=1024):
    rows, count = kerns[0].shape[0], len(kerns)
    half, rhs = runs[0].shape[1], runs[0].shape[2] // parts

    def kernel(table_ref, *refs):
        base_ref, theirs_ref, mine_ref, c_ref = refs[count + len(runs):]
        col = table_ref[len(slots)]
        span = pl.ds(pl.multiple_of(col * rhs, rhs), rhs)

        def store(at, value):
            theirs_ref[at] = value[:, :rhs]
            mine_ref[at] = base_ref[at, span] - value[:, rhs:]

        product(refs[:count], slots, table_ref, refs[count:count + len(runs)], (parts - 1 - col, col), c_ref, tile, store)

    scratch = (len(slots) * half, 4 * rhs)
    return call(
        kernel, kerns, runs, [residual], table, (2, (rows, rhs)), scratch, 6 * rows * scratch[0] * 2 * rhs
    )


def apply_far(kerns, slots, runs, table, base, mine, parts, tile=1024):
    rows, count = kerns[0].shape[0], len(kerns)
    half, rhs = runs[0].shape[1], runs[0].shape[2] // parts

    def kernel(table_ref, *refs):
        base_ref, out_ref, c_ref = refs[count + len(runs):]
        col = table_ref[len(slots)]

        def store(at, value):
            out_ref[at] = base_ref[at] - value if mine else base_ref[at] + value

        cols = (col if mine else parts - 1 - col,)
        product(refs[:count], slots, table_ref, refs[count:count + len(runs)], cols, c_ref, tile, store)

    scratch = (len(slots) * half, 2 * rhs)
    return call(kernel, kerns, runs, [base], table, (1, (rows, rhs)), scratch, 6 * rows * scratch[0] * rhs)[0]


def moves(depth):
    steps, held = [], {"own": {z: z for z in range(depth)}}

    def step(name, pairs, source):
        pairs = [(s, d) for s, d in pairs if s in held[source]]
        held[name] = {d: held[source][s] for s, d in pairs}
        steps.append((name, pairs, source))

    if depth == 4:
        inner, outer = [(1, 2), (2, 1)], [(1, 0), (2, 3)]
        step("a", [(0, 1), (1, 0), (2, 3), (3, 2)], "own")
        step("b", inner, "own")
        step("c", inner, "a")
        step("d", outer, "b")
        step("e", outer, "c")
    else:
        up = down = "own"
        for s in range(1, depth):
            step(f"u{s}", [(z, z + 1) for z in range(depth - 1)], up)
            step(f"d{s}", [(z, z - 1) for z in range(1, depth)], down)
            up, down = f"u{s}", f"d{s}"
    order = [name for name, _, _ in steps]
    slots = []
    for z in range(depth):
        slots.append([(name, held[name][z]) for name in order if z in held[name]])
    return steps, slots


def permute(x, pairs):
    return lax.ppermute(x, "row", pairs)


def along(pairs):
    return [(s * WIDTH + y, d * WIDTH + y) for s, d in pairs for y in range(WIDTH)]


def on_device(inverse, features, residual, block_ids):
    n = lax.axis_size("row")
    depth = n // WIDTH
    col, cols = lax.axis_index("col"), lax.axis_size("col")
    z = lax.shift_right_logical(lax.axis_index("row"), 1)
    across = [(r, r ^ 1) for r in range(n)]
    half = block_ids.shape[0] // cols

    own = gather(features, block_ids, half)
    steps, slots = moves(depth)

    places, masks = [z], []
    for j in range(depth - 1):
        by_name, place = {}, jnp.int32(0)
        for zz in range(depth):
            by_name.setdefault(slots[zz][j][0], []).append(zz)
            place = jnp.where(z == zz, slots[zz][j][1], place)
        places.append(place)
        masks.append({name: any_of(z, zs) for name, zs in list(by_name.items())})
    ends = [(z == i) | (z == depth - 1 - i) for i in range(depth // 2 - 1)]
    table = jnp.stack(places + [col]).astype(jnp.int32)
    own, masks, ends, table = lax.optimization_barrier((own, masks, ends, table))

    bufs = {"own": own}
    for name, pairs, source in steps:
        bufs[name] = permute(bufs[source], along(pairs))

    res = gather(residual, block_ids, block_ids.shape[0])
    send, keep = partial(inverse.reshape(n, half, -1), res, RUNS)

    sames, crosses = [], []
    for h in range(RUNS):
        term = keep[h] + permute(send[h], across)
        inward = [[(s, s + 1), (depth - 1 - s, depth - 2 - s)] for s in range(depth // 2 - 1)]
        for pairs in inward:
            term = term + permute(term, along(pairs))
        pairs = [(depth // 2 - 1, depth // 2), (depth // 2, depth // 2 - 1)]
        term = term + permute(term, along(pairs))
        for i, pairs in reversed(list(enumerate(inward))):
            back = permute(term, along([(d, s) for s, d in pairs]))
            term = jnp.where(ends[i], back, term)
        sames.append(term)
        crosses.append(permute(term, across))

    x_high, x_low = split(features)
    nears, fars = [], []
    for j in range(depth):
        block = own
        if j > 0:
            block = None
            for name, mask in masks[j - 1].items():
                block = bufs[name] if block is None else jnp.where(mask, bufs[name], block)
        nears.append(block)
        if j == 1 and depth == 4:
            fars.append(permute(fars[0], along(steps[0][1])))
        else:
            fars.append(permute(block, across))
    near_slots = list(range(depth))
    far_slots = [0, 2, 1, 3] if depth == 4 else near_slots
    near_kerns, far_kerns = [], []
    for i in range(0, depth, 2):
        near_kerns += gram(x_high, x_low, *[nears[j] for j in near_slots[i:i + 2]])
        far_kerns += gram(x_high, x_low, *[fars[j] for j in far_slots[i:i + 2]])

    theirs, mine = apply_near(near_kerns, near_slots, sames, table, residual, cols)
    theirs = apply_far(far_kerns, far_slots, crosses, table, theirs, False, cols)
    got = lax.ppermute(theirs, "col", [(c, cols - 1 - c) for c in range(cols)])
    mine = apply_far(far_kerns, far_slots, crosses, table, mine, True, cols)
    return mine - got


def any_of(z, places):
    mask = z == places[0]
    for p in places[1:]:
        mask = mask | (z == p)
    return mask


def solution(mesh):
    return jax.shard_map(
        on_device,
        mesh=mesh,
        in_specs=(
            P("groups", "col", None, "row"),
            P(("groups", "row"), None),
            P(("groups", "row"), None),
            P(("groups", "row")),
        ),
        out_specs=P(("groups", "row"), "col"),
        check_vma=False,
    )
```

```python
import jax
import jax.numpy as jnp
from jax import lax
from jax.experimental import pallas as pl
from jax.experimental.pallas import tpu as pltpu
from jax.sharding import PartitionSpec as P

F32, BF16 = jnp.float32, jnp.bfloat16
NT = (((1,), (1,)), ((), ()))
NN = (((1,), (0,)), ((), ()))
WIDTH = 2
RUNS = 2


def mm(a, b, dims):
    return lax.dot_general(a, b, dims, preferred_element_type=F32)


def halves(x):
    high = x.astype(BF16)
    return high, (x - high.astype(F32)).astype(BF16)


VMEM = pl.BlockSpec(memory_space=pltpu.VMEM)
PARAMS = pltpu.CompilerParams(vmem_limit_bytes=8 << 20)


def in_vmem(*arrays):
    return [pltpu.with_memory_space_constraint(a, pltpu.VMEM) for a in arrays]


def split_kernel(x_ref, high_ref, low_ref):
    high_ref[...], low_ref[...] = halves(x_ref[...])


def split(x, tile=256):
    rows, cols = x.shape
    return pl.pallas_call(
        split_kernel,
        grid=(rows // tile,),
        in_specs=[pl.BlockSpec((tile, cols), lambda i: (i, 0))],
        out_specs=[pl.BlockSpec((tile, cols), lambda i: (i, 0))] * 2,
        out_shape=[pltpu.VMEM(x.shape, BF16)] * 2,
        compiler_params=PARAMS,
        cost_estimate=pl.CostEstimate(flops=4 * rows * cols, bytes_accessed=8 * rows * cols, transcendentals=0),
    )(x)


def gather_kernel(whole, ids_hbm, x_ref, out_ref, ids_ref, ids_sem, sem):
    copy = pltpu.make_async_copy(ids_hbm, ids_ref, ids_sem)
    copy.start()
    copy.wait()
    count = out_ref.shape[0]
    first = 0 if whole else lax.axis_index("col") * count
    base = lax.axis_index("row") * x_ref.shape[0]

    @pl.loop(0, count, unroll=8)
    def _(i):
        row = ids_ref[first + i] - base
        pltpu.make_async_copy(x_ref.at[pl.ds(row, 1)], out_ref.at[pl.ds(i, 1)], sem).start()

    pltpu.make_async_copy(x_ref.at[pl.ds(0, count)], out_ref, sem).wait()


def gather(x, ids, count):
    return pl.pallas_call(
        lambda *refs: gather_kernel(count == ids.shape[0], *refs),
        in_specs=[pl.BlockSpec(memory_space=pltpu.HBM)] * 2,
        out_specs=VMEM,
        out_shape=jax.ShapeDtypeStruct((count, x.shape[1]), x.dtype),
        scratch_shapes=[pltpu.SMEM(ids.shape, ids.dtype), pltpu.SemaphoreType.DMA, pltpu.SemaphoreType.DMA],
        compiler_params=PARAMS,
        cost_estimate=pl.CostEstimate(flops=0, bytes_accessed=8 * count * x.shape[1], transcendentals=0),
    )(*[pltpu.with_memory_space_constraint(a, pltpu.HBM) for a in (ids, x)])


def partial_kernel(runs, inv_ref, res_ref, *out_refs):
    y = lax.rem(lax.axis_index("row"), WIDTH)
    high, low = halves(res_ref[...])
    for i, ref in enumerate(out_refs):
        run, side = i % runs, i // runs
        for k in range(ref.shape[0]):
            place = (run * ref.shape[0] + k) * WIDTH
            ih, il = halves(inv_ref[place + (y if side else 1 - y)])
            ref[k] = mm(ih, low, NN) + mm(il, high, NN) + mm(ih, high, NN)


def partial(inverse, res, runs):
    blocks, half, mine = inverse.shape
    shape = (blocks // WIDTH // runs, half, res.shape[1])
    outs = pl.pallas_call(
        lambda *refs: partial_kernel(runs, *refs),
        in_specs=[VMEM, VMEM],
        out_specs=[VMEM] * (2 * runs),
        out_shape=[jax.ShapeDtypeStruct(shape, F32)] * (2 * runs),
        compiler_params=PARAMS,
        cost_estimate=pl.CostEstimate(
            flops=6 * blocks * half * mine * res.shape[1], bytes_accessed=8 * blocks * half * mine, transcendentals=0
        ),
    )(inverse, res)
    return outs[:runs], outs[runs:]


def gram_kernel(scale, tile, xh_ref, xl_ref, *refs):
    blocks, (kh_ref, kl_ref, ph_ref, pl_ref) = refs[:-4], refs[-4:]
    half = blocks[0].shape[0]
    for i, ref in enumerate(blocks):
        rows = slice(i * half, (i + 1) * half)
        ph_ref[rows], pl_ref[rows] = halves(ref[...])
    for r in range(0, kh_ref.shape[0], tile):
        rows = slice(r, r + tile)
        xh, ph = xh_ref[rows], ph_ref[...]
        gram = mm(xh, pl_ref[...], NT) + mm(xl_ref[rows], ph, NT) + mm(xh, ph, NT)
        root = gram * scale + 0.5
        kh_ref[rows], kl_ref[rows] = halves(root * root)


def gram(x_high, x_low, *blocks, tile=1024):
    rows, feats = x_high.shape
    points = len(blocks) * blocks[0].shape[0]
    return pl.pallas_call(
        lambda *refs: gram_kernel(1.0 / feats, tile, *refs),
        in_specs=[VMEM] * (2 + len(blocks)),
        out_specs=[VMEM] * 2,
        out_shape=[pltpu.VMEM((rows, points), BF16)] * 2,
        scratch_shapes=[pltpu.VMEM((points, feats), BF16)] * 2,
        compiler_params=PARAMS,
        cost_estimate=pl.CostEstimate(
            flops=6 * rows * feats * points, bytes_accessed=4 * rows * (feats + points), transcendentals=0
        ),
    )(*in_vmem(x_high, x_low), *blocks)


def fill(c_ref, row, ref, place, cols):
    half, rhs = ref.shape[1], c_ref.shape[1] // 2 // len(cols)
    rows = pl.ds(row, half)
    for i, col in enumerate(cols):
        span = pl.ds(pl.multiple_of(col * rhs, rhs), rhs)
        high, low = halves(ref[place, :, span])
        c_ref[rows, i * rhs:(i + 1) * rhs] = high
        c_ref[rows, (len(cols) + i) * rhs:(len(cols) + i + 1) * rhs] = low


def product(kerns, slots, places, run_refs, cols, c_ref, tile, store):
    each, half = run_refs[0].shape[:2]
    for i, slot in enumerate(slots):
        place = places[slot]
        for r, ref in enumerate(run_refs):

            @pl.when((place >= r * each) & (place < (r + 1) * each))
            def _():
                fill(c_ref, i * half, ref, place - r * each, cols)

    width = c_ref.shape[1] // 2
    for r in range(0, kerns[0].shape[0], tile):
        span = slice(r, r + tile)
        high = jnp.concatenate([ref[span] for ref in kerns[::2]], 1)
        low = jnp.concatenate([ref[span] for ref in kerns[1::2]], 1)
        both = mm(high, c_ref[...], NN)
        store(span, both[:, :width] + (both[:, width:] + mm(low, c_ref[:, :width], NN)))


def call(kernel, kerns, runs, others, table, outs, scratch, cost):
    return pl.pallas_call(
        kernel,
        in_specs=[pl.BlockSpec(memory_space=pltpu.SMEM)] + [VMEM] * (len(kerns) + len(runs) + len(others)),
        out_specs=[VMEM] * outs[0],
        out_shape=[pltpu.VMEM(outs[1], F32)] * outs[0],
        scratch_shapes=[pltpu.VMEM(scratch, BF16)],
        compiler_params=PARAMS,
        cost_estimate=pl.CostEstimate(flops=cost, bytes_accessed=cost // 1024, transcendentals=0),
    )(table, *in_vmem(*kerns), *runs, *in_vmem(*others))


def apply_near(kerns, slots, runs, table, residual, parts, tile=1024):
    rows, count = kerns[0].shape[0], len(kerns)
    half, rhs = runs[0].shape[1], runs[0].shape[2] // parts

    def kernel(table_ref, *refs):
        base_ref, theirs_ref, mine_ref, c_ref = refs[count + len(runs):]
        col = table_ref[len(slots)]
        span = pl.ds(pl.multiple_of(col * rhs, rhs), rhs)

        def store(at, value):
            theirs_ref[at] = value[:, :rhs]
            mine_ref[at] = base_ref[at, span] - value[:, rhs:]

        product(refs[:count], slots, table_ref, refs[count:count + len(runs)], (parts - 1 - col, col), c_ref, tile, store)

    scratch = (len(slots) * half, 4 * rhs)
    return call(
        kernel, kerns, runs, [residual], table, (2, (rows, rhs)), scratch, 6 * rows * scratch[0] * 2 * rhs
    )


def apply_far(kerns, slots, runs, table, base, mine, parts, tile=1024):
    rows, count = kerns[0].shape[0], len(kerns)
    half, rhs = runs[0].shape[1], runs[0].shape[2] // parts

    def kernel(table_ref, *refs):
        base_ref, out_ref, c_ref = refs[count + len(runs):]
        col = table_ref[len(slots)]

        def store(at, value):
            out_ref[at] = base_ref[at] - value if mine else base_ref[at] + value

        cols = (col if mine else parts - 1 - col,)
        product(refs[:count], slots, table_ref, refs[count:count + len(runs)], cols, c_ref, tile, store)

    scratch = (len(slots) * half, 2 * rhs)
    return call(kernel, kerns, runs, [base], table, (1, (rows, rhs)), scratch, 6 * rows * scratch[0] * rhs)[0]


def moves(depth):
    steps, held = [], {"own": {z: z for z in range(depth)}}

    def step(name, pairs, source):
        pairs = [(s, d) for s, d in pairs if s in held[source]]
        held[name] = {d: held[source][s] for s, d in pairs}
        steps.append((name, pairs, source))

    if depth == 4:
        inner, outer = [(1, 2), (2, 1)], [(1, 0), (2, 3)]
        step("a", [(0, 1), (1, 0), (2, 3), (3, 2)], "own")
        step("b", inner, "own")
        step("c", inner, "a")
        step("d", outer, "b")
        step("e", outer, "c")
    else:
        up = down = "own"
        for s in range(1, depth):
            step(f"u{s}", [(z, z + 1) for z in range(depth - 1)], up)
            step(f"d{s}", [(z, z - 1) for z in range(1, depth)], down)
            up, down = f"u{s}", f"d{s}"
    order = [name for name, _, _ in steps]
    slots = []
    for z in range(depth):
        slots.append([(name, held[name][z]) for name in order if z in held[name]])
    return steps, slots


def permute(x, pairs):
    return lax.ppermute(x, "row", pairs)


def along(pairs):
    return [(s * WIDTH + y, d * WIDTH + y) for s, d in pairs for y in range(WIDTH)]


def on_device(inverse, features, residual, block_ids):
    n = lax.axis_size("row")
    depth = n // WIDTH
    col, cols = lax.axis_index("col"), lax.axis_size("col")
    z = lax.shift_right_logical(lax.axis_index("row"), 1)
    across = [(r, r ^ 1) for r in range(n)]
    half = block_ids.shape[0] // cols

    own = gather(features, block_ids, half)
    steps, slots = moves(depth)

    places, masks = [z], []
    for j in range(depth - 1):
        by_name, place = {}, jnp.int32(0)
        for zz in range(depth):
            by_name.setdefault(slots[zz][j][0], []).append(zz)
            place = jnp.where(z == zz, slots[zz][j][1], place)
        places.append(place)
        masks.append({name: any_of(z, zs) for name, zs in list(by_name.items())})
    ends = [(z == i) | (z == depth - 1 - i) for i in range(depth // 2 - 1)]
    table = jnp.stack(places + [col]).astype(jnp.int32)
    own, masks, ends, table = lax.optimization_barrier((own, masks, ends, table))

    bufs = {"own": own}
    for name, pairs, source in steps:
        bufs[name] = permute(bufs[source], along(pairs))

    res = gather(residual, block_ids, block_ids.shape[0])
    send, keep = partial(inverse.reshape(n, half, -1), res, RUNS)

    sames, crosses = [], []
    for h in range(RUNS):
        term = keep[h] + permute(send[h], across)
        inward = [[(s, s + 1), (depth - 1 - s, depth - 2 - s)] for s in range(depth // 2 - 1)]
        for pairs in inward:
            term = term + permute(term, along(pairs))
        pairs = [(depth // 2 - 1, depth // 2), (depth // 2, depth // 2 - 1)]
        term = term + permute(term, along(pairs))
        for i, pairs in reversed(list(enumerate(inward))):
            back = permute(term, along([(d, s) for s, d in pairs]))
            term = jnp.where(ends[i], back, term)
        sames.append(term)
        crosses.append(permute(term, across))

    x_high, x_low = split(features)
    nears, fars = [], []
    for j in range(depth):
        block = own
        if j > 0:
            block = None
            for name, mask in masks[j - 1].items():
                block = bufs[name] if block is None else jnp.where(mask, bufs[name], block)
        nears.append(block)
        if j == 1 and depth == 4:
            fars.append(permute(fars[0], along(steps[0][1])))
        else:
            fars.append(permute(block, across))
    near_slots = list(range(depth))
    far_groups = [[0, 2], [3], [1]] if depth == 4 else [[j, j + 1] for j in range(0, depth, 2)]
    far_slots = sum(far_groups, [])
    near_kerns, far_kerns = [], []
    for i in range(0, depth, 2):
        near_kerns += gram(x_high, x_low, *[nears[j] for j in near_slots[i:i + 2]])
    for group in far_groups:
        far_kerns += gram(x_high, x_low, *[fars[j] for j in group])

    theirs, mine = apply_near(near_kerns, near_slots, sames, table, residual, cols)
    theirs = apply_far(far_kerns, far_slots, crosses, table, theirs, False, cols)
    got = lax.ppermute(theirs, "col", [(c, cols - 1 - c) for c in range(cols)])
    mine = apply_far(far_kerns, far_slots, crosses, table, mine, True, cols)
    return mine - got


def any_of(z, places):
    mask = z == places[0]
    for p in places[1:]:
        mask = mask | (z == p)
    return mask


def solution(mesh):
    return jax.shard_map(
        on_device,
        mesh=mesh,
        in_specs=(
            P("groups", "col", None, "row"),
            P(("groups", "row"), None),
            P(("groups", "row"), None),
            P(("groups", "row")),
        ),
        out_specs=P(("groups", "row"), "col"),
        check_vma=False,
    )
```
